256 devices in a mesh: pos: 8 (over z_hi, core), rows: 32 (over z_lo, x, y).
Axes of the slice: x: 4, y: 4, z: 8 (z_hi: 4, z_lo: 2; z = z_hi * 2 + z_lo), core: 2. Of those that a mesh axis runs over, the one named last changes fastest.
Arguments:
- matrix: float32 [16384, 2048], P('rows', 'pos'), may hold values from -40 to 40
- shifts: int32 [3], replicated, may hold values from 1 to 31, as said below
Outputs:
- rotated: float32 [16384, 2048], P('rows', 'pos')
The draws below stay inside these ranges and needn't reach their ends.
Inputs may be any that keep to these rules, and one draw needn't show every extreme that they name: `shifts`: each entry is a distance between pair positions, taken modulo 8; 31 and 7 both occur in every draw.
All inputs are finite; a program needn't handle non-finite values. Where the reference program divides by a largest or mean magnitude, that divisor is 1e-20 or more.
Results may differ from the reference program's by a relative error of at most 0.00018.
Values sent between devices are 32-bit elements; how exact they have to be, the bound alone decides.
A program may use at most 64 MiB of HBM per device.

```python
import jax
import jax.numpy as jnp
from jax import lax

BLK = 128
ROW_DEV = 512
ROUNDS = 3
NS_STEPS = 3
N_POS = 8
N_ROWS = 32


def draw_matrix(key, part):
    keys = jax.random.split(jax.random.fold_in(key, 11), 4)
    total_rows = ROW_DEV * N_ROWS
    total_cols = 2 * BLK * N_POS
    col_scale = jnp.exp(jax.random.uniform(keys[0], (1, total_cols), jnp.float32, jnp.log(0.3), jnp.log(3.0)))
    factor_rows = jnp.clip(jax.random.normal(keys[1], (total_rows, 1), jnp.float32), -3.0, 3.0)
    factor_cols = jnp.clip(jax.random.normal(keys[2], (1, total_cols), jnp.float32), -3.0, 3.0)
    noise = jnp.clip(jax.random.normal(keys[3], (total_rows, total_cols), jnp.float32), -4.0, 4.0)
    common = 0.7
    return col_scale * (noise + common * factor_rows * factor_cols)


def draw_shifts(key, part):
    keys = jax.random.split(jax.random.fold_in(key, 23), 2)
    values = jax.random.randint(keys[0], (ROUNDS,), 1, 4 * N_POS)
    order = jax.random.permutation(keys[1], ROUNDS)
    slots = jnp.arange(ROUNDS)
    values = jnp.where(slots == order[0], 4 * N_POS - 1, values)
    values = jnp.where(slots == order[1], N_POS - 1, values)
    return values.astype(jnp.int32)


def setup_inputs(seed: int = 0) -> dict:
    key_list = jax.random.split(jax.random.key(seed), 3)
    matrix = draw_matrix(jax.random.fold_in(key_list[2], 71), 0)
    shifts = draw_shifts(jax.random.fold_in(key_list[2], 71), 0)
    return dict(matrix=matrix, shifts=shifts)


def product(left, right):
    return jnp.dot(left, right, precision=lax.Precision.HIGHEST, preferred_element_type=jnp.float32)

def rotation(gram_matrix):
    width = gram_matrix.shape[0]
    identity = jnp.eye(width, dtype=gram_matrix.dtype)
    inverse_norm = 1.0 / jnp.sqrt(jnp.diagonal(gram_matrix) + 1e-06)
    scaled = gram_matrix * inverse_norm[:, None] * inverse_norm[None, :]
    upper = jnp.triu(scaled, 1)
    skew_raw = upper - upper.T
    bound_value = jnp.max(lax.optimization_barrier(jnp.sum(jnp.abs(skew_raw), axis=1)))
    skew = skew_raw / (1.0 + 2.0 * bound_value)
    shifted = identity - skew
    inverse = identity + skew
    for step in range(NS_STEPS):
        inverse = product(inverse, 2.0 * identity - product(shifted, inverse))
    return product(inverse, identity + skew)

def one_position(block):
    gram_matrix = product(block.T, block)
    return product(block, rotation(gram_matrix))

def reference(matrix, shifts):
    rows_total = matrix.shape[0]
    current = matrix.reshape(rows_total, N_POS, 2 * BLK).transpose(1, 0, 2)
    for round_index in range(ROUNDS):
        current = lax.map(one_position, current)
        moved = jnp.roll(current[:, :, BLK:], shifts[round_index], axis=0)
        current = jnp.concatenate([current[:, :, :BLK], moved], axis=2)
    return current.transpose(1, 0, 2).reshape(rows_total, N_POS * 2 * BLK)
```

```python
import functools

import jax
import jax.numpy as jnp
from jax import lax
from jax.experimental import pallas as pl
from jax.experimental.pallas import tpu as pltpu
from jax.sharding import PartitionSpec as P

ROUNDS = 3
COMMON = 7
BLK = 128
TILE = 8
CHUNKS = 4
MESH = pl.DeviceIdType.MESH
F32 = jnp.float32
BF16 = jnp.bfloat16


def split(x):
    high = x.astype(BF16)
    return high, (x - high.astype(F32)).astype(BF16)


def mm(a, b):
    return jnp.dot(a, b, preferred_element_type=F32)


def mm3(a, b_high, b_low):
    a_high, a_low = split(a)
    return mm(a_high, b_high) + (mm(a_low, b_high) + mm(a_high, b_low))


def mm_t(a, b):
    return lax.dot_general(a, b, (((0,), (0,)), ((), ())), preferred_element_type=F32)


def triangle_masks():
    row = lax.broadcasted_iota(jnp.int32, (BLK, BLK), 0)
    col = lax.broadcasted_iota(jnp.int32, (BLK, BLK), 1)
    return row < col, row > col, row == col


def pack_gram(gram, out):
    upper, lower, diag = triangle_masks()
    g11, g12, g22 = gram[:BLK, :BLK], gram[:BLK, BLK:], gram[BLK:, BLK:]
    out[0:BLK, :] = g12
    out[BLK : 2 * BLK, :] = jnp.where(lower, g22, g11)
    diag2 = jnp.sum(jnp.where(diag, g22, 0.0), axis=0, keepdims=True)
    out[2 * BLK :, :] = jnp.broadcast_to(diag2, (TILE, BLK))


def cayley_less_identity(summed):
    upper, lower, diag = triangle_masks()
    g12 = summed[0:BLK, :]
    both = summed[BLK : 2 * BLK, :]
    d2_row = summed[2 * BLK : 2 * BLK + 1, :]
    d1 = jnp.where(diag, both, 0.0)
    d2 = jnp.where(diag, jnp.broadcast_to(d2_row, (BLK, BLK)), 0.0)

    def inv(x):
        return 1.0 / jnp.sqrt(x + 1e-06)

    n1_row = inv(jnp.sum(d1, axis=0, keepdims=True))
    n1_col = inv(jnp.sum(d1, axis=1, keepdims=True))
    n2_row = inv(d2_row)
    n2_col = inv(jnp.sum(d2, axis=1, keepdims=True))
    s12 = g12 * n1_col * n2_row
    up11 = jnp.where(upper, both * n1_col * n1_row, 0.0)
    low22 = jnp.where(lower, both * n2_col * n2_row, 0.0)
    raw11 = up11 - up11.T
    raw22 = low22.T - low22
    raw = jnp.concatenate(
        [
            jnp.concatenate([raw11, s12], axis=1),
            jnp.concatenate([-s12.T, raw22], axis=1),
        ],
        axis=0,
    )
    sums = jnp.sum(jnp.abs(raw), axis=0, keepdims=True)
    bound = jnp.max(sums, axis=1, keepdims=True)
    skew = raw * (1.0 / (1.0 + 2.0 * bound))
    s_h, s_l = split(skew)
    y = mm(s_h, s_h) + (mm(s_l, s_h) + mm(s_h, s_l))
    y_h, y_l = split(y)
    w = 2.0 * skew + y
    z = mm(y_h, y_h) + (mm(y_l, y_h) + mm(y_h, y_l))
    q1 = w + y + mm3(w, y_h, y_l)
    z_h, z_l = split(z)
    v = mm(z_h, z_h) + (mm(z_l, z_h) + mm(z_h, z_l))
    q2 = q1 + z + mm3(q1, z_h, z_l)
    v_h, v_l = split(v)
    return q2 + v + mm3(q2, v_h, v_l)


def kernel(distances, n_pos, n_rows, x_hbm, out_hbm, a, b, s, pack, part, summed,
           d_high, d_low, load_sem, in_sem, send_sem, part_send, part_recv, sum_send,
           sum_recv, out_sem):
    me = lax.axis_index("rows")
    pos = lax.axis_index("pos")
    last = n_rows - 1
    height = a.shape[0]
    step = height // CHUNKS
    barrier = pltpu.get_barrier_semaphore()

    load_a = pltpu.make_async_copy(x_hbm.at[:, pl.ds(0, BLK)], a, load_sem)
    load_a.start()
    for c in range(CHUNKS):
        rows = pl.ds(c * step, step)
        pltpu.make_async_copy(
            x_hbm.at[rows, pl.ds(BLK, BLK)], b.at[0, rows], in_sem.at[0, c]
        ).start()

    @pl.loop(1, n_rows)
    def _(d):
        pl.semaphore_signal(
            barrier, inc=1, device_id={"rows": lax.rem(me + d, n_rows)}, device_id_type=MESH
        )

    @pl.loop(1, n_pos)
    def _(d):
        pl.semaphore_signal(
            barrier, inc=1, device_id={"pos": lax.rem(pos + d, n_pos)}, device_id_type=MESH
        )

    load_a.wait()

    def send_part(r, d, peer, size):
        pltpu.make_async_remote_copy(
            src_ref=pack.at[r, pl.ds(pl.multiple_of(peer * TILE, TILE), size)],
            dst_ref=part.at[r, pl.ds(pl.multiple_of((d - 1) * size, TILE), size)],
            send_sem=part_send.at[r],
            recv_sem=part_recv.at[r],
            device_id={"rows": peer},
            device_id_type=MESH,
        ).start()

    def send_sum(r, peer, size):
        rows = pl.ds(pl.multiple_of(me * TILE, TILE), size)
        pltpu.make_async_remote_copy(
            src_ref=summed.at[r, rows],
            dst_ref=summed.at[r, rows],
            send_sem=sum_send.at[r],
            recv_sem=sum_recv.at[r],
            device_id={"rows": peer},
            device_id_type=MESH,
        ).start()

    def wait_rows(r, count, sem):
        ref = part.at[r, pl.ds(0, count)]
        pltpu.make_async_copy(ref, ref, sem.at[r]).wait()

    def add_parts(r, size):
        rows = pl.ds(pl.multiple_of(me * TILE, TILE), size)
        terms = [pack[r, rows, :]]
        for d in range(n_rows - 1):
            terms.append(part[r, pl.ds(d * size, size), :])
        while len(terms) > 1:
            terms = [sum(terms[i : i + 2]) for i in range(0, len(terms), 2)]
        summed[r, rows, :] = terms[0]

    def one_round(r, carry):
        gram = None
        cross = None
        for c in range(CHUNKS):
            rows = pl.ds(c * step, step)
            pltpu.make_async_copy(b.at[r, rows], b.at[r, rows], in_sem.at[r, c]).wait()
            x_h, x_l = split(jnp.concatenate([a[rows, :], b[r, rows, :]], axis=1))
            hh, hl = mm_t(x_h, x_h), mm_t(x_h, x_l)
            gram = hh if c == 0 else gram + hh
            cross = hl if c == 0 else cross + hl
        pack_gram(gram + (cross + cross.T), pack.at[r])

        @pl.when(r == 0)
        def _():
            pl.semaphore_wait(barrier, n_rows - 1 + n_pos - 1)

        @pl.loop(1, n_rows)
        def _(d):
            peer = lax.rem(me + d, n_rows)

            @pl.when(peer != last)
            def _():
                send_part(r, d, peer, TILE)

            @pl.when(peer == last)
            def _():
                send_part(r, d, peer, 2 * TILE)

        @pl.when(me != last)
        def _():
            wait_rows(r, (n_rows - 1) * TILE, part_recv)
            add_parts(r, TILE)

            @pl.loop(1, n_rows)
            def _(d):
                send_sum(r, lax.rem(me + d, n_rows), TILE)

            wait_rows(r, n_rows * TILE, part_send)
            wait_rows(r, n_rows * TILE, sum_recv)
            wait_rows(r, (n_rows - 1) * TILE, sum_send)

        @pl.when(me == last)
        def _():
            wait_rows(r, (n_rows - 1) * 2 * TILE, part_recv)
            add_parts(r, 2 * TILE)

            @pl.loop(1, n_rows)
            def _(d):
                send_sum(r, lax.rem(me + d, n_rows), 2 * TILE)

            wait_rows(r, (n_rows - 1) * TILE, part_send)
            wait_rows(r, (n_rows - 1) * TILE, sum_recv)
            wait_rows(r, (n_rows - 1) * 2 * TILE, sum_send)

        delta = cayley_less_identity(summed.at[r])
        high, low = split(delta)
        d_high[...] = high
        d_low[...] = low

        distance = COMMON
        for i, value in enumerate(distances):
            distance = jnp.where(r == i, value, distance)
        target = lax.rem(pos + distance, n_pos)
        for c in range(CHUNKS):
            rows = pl.ds(c * step, step)
            x = jnp.concatenate([a[rows, :], b[r, rows, :]], axis=1)
            x_h, x_l = split(x)
            x = x + (
                mm(x_h, d_high[...]) + (mm(x_l, d_high[...]) + mm(x_h, d_low[...]))
            )
            a[rows, :] = x[:, :BLK]
            s[r, rows, :] = x[:, BLK:]

            def send():
                pltpu.make_async_remote_copy(
                    src_ref=s.at[r, rows],
                    dst_ref=b.at[r + 1, rows],
                    send_sem=send_sem.at[r, c],
                    recv_sem=in_sem.at[r + 1, c],
                    device_id={"pos": target},
                    device_id_type=MESH,
                ).start()

            def keep():
                pltpu.make_async_copy(
                    s.at[r, rows], b.at[r + 1, rows], in_sem.at[r + 1, c]
                ).start()

            if 0 in distances:
                stays = distances.index(0)
                pl.when(r == stays)(keep)
                pl.when(r != stays)(send)
            else:
                send()
        return carry

    lax.fori_loop(0, ROUNDS, one_round, 0)

    out_a = pltpu.make_async_copy(a, out_hbm.at[:, pl.ds(0, BLK)], out_sem.at[CHUNKS])
    out_a.start()
    for c in range(CHUNKS):
        rows = pl.ds(c * step, step)
        pltpu.make_async_copy(
            b.at[ROUNDS, rows], b.at[ROUNDS, rows], in_sem.at[ROUNDS, c]
        ).wait()
        pltpu.make_async_copy(
            b.at[ROUNDS, rows], out_hbm.at[rows, pl.ds(BLK, BLK)], out_sem.at[c]
        ).start()
    for r in range(ROUNDS):
        if distances[r] != 0:
            for c in range(CHUNKS):
                rows = pl.ds(c * step, step)
                pltpu.make_async_copy(s.at[r, rows], s.at[r, rows], send_sem.at[r, c]).wait()
    for c in range(CHUNKS):
        rows = pl.ds(c * step, step)
        pltpu.make_async_copy(
            b.at[ROUNDS, rows], out_hbm.at[rows, pl.ds(BLK, BLK)], out_sem.at[c]
        ).wait()
    out_a.wait()


def make_branch(distances, identity, n_pos, n_rows, height):
    call = pl.pallas_call(
        functools.partial(kernel, distances, n_pos, n_rows),
        out_shape=jax.ShapeDtypeStruct((height, 2 * BLK), F32),
        in_specs=[pl.BlockSpec(memory_space=pl.ANY)],
        out_specs=pl.BlockSpec(memory_space=pl.ANY),
        scratch_shapes=[
            pltpu.VMEM((height, BLK), F32),
            pltpu.VMEM((ROUNDS + 1, height, BLK), F32),
            pltpu.VMEM((ROUNDS, height, BLK), F32),
            pltpu.VMEM((ROUNDS, 2 * BLK + TILE, BLK), F32),
            pltpu.VMEM((ROUNDS, n_rows * 2 * TILE, BLK), F32),
            pltpu.VMEM((ROUNDS, 2 * BLK + TILE, BLK), F32),
            pltpu.VMEM((2 * BLK, 2 * BLK), BF16),
            pltpu.VMEM((2 * BLK, 2 * BLK), BF16),
            pltpu.SemaphoreType.DMA,
            pltpu.SemaphoreType.DMA((ROUNDS + 1, CHUNKS)),
            pltpu.SemaphoreType.DMA((ROUNDS, CHUNKS)),
            pltpu.SemaphoreType.DMA((ROUNDS,)),
            pltpu.SemaphoreType.DMA((ROUNDS,)),
            pltpu.SemaphoreType.DMA((ROUNDS,)),
            pltpu.SemaphoreType.DMA((ROUNDS,)),
            pltpu.SemaphoreType.DMA((CHUNKS + 1,)),
        ],
        compiler_params=pltpu.CompilerParams(
            collective_id=identity, has_side_effects=True, vmem_limit_bytes=32 << 20
        ),
    )
    return call


def solution(mesh):
    n_pos, n_rows = mesh.shape["pos"], mesh.shape["rows"]
    common = COMMON % n_pos
    plans = [
        tuple(value if i == odd else common for i in range(ROUNDS))
        for odd in range(ROUNDS)
        for value in range(n_pos - 1)
    ]
    plans.append((common,) * ROUNDS)

    def shards(matrix, shifts):
        moved = shifts % n_pos
        other = moved != common
        odd = jnp.argmax(other)
        plan = jnp.where(jnp.any(other), odd * (n_pos - 1) + moved[odd], len(plans) - 1)
        branches = [
            make_branch(distances, i, n_pos, n_rows, matrix.shape[0])
            for i, distances in enumerate(plans)
        ]
        return lax.switch(plan, branches, matrix)

    return jax.shard_map(
        shards, mesh=mesh, in_specs=(P("rows", "pos"), P()), out_specs=P("rows", "pos"),
        check_vma=False,
    )
```

```python
import functools

import jax
import jax.numpy as jnp
from jax import lax
from jax.experimental import pallas as pl
from jax.experimental.pallas import tpu as pltpu
from jax.sharding import PartitionSpec as P

ROUNDS = 3
NS_STEPS = 3
COMMON = 7
BLK = 128
TILE = 8
CHUNKS = 4
BLOCKS = 3
SIDE = 4
NEAR = 15
MESH = pl.DeviceIdType.MESH
F32 = jnp.float32
BF16 = jnp.bfloat16
FIRST, SECOND = slice(0, BLK), slice(BLK, 2 * BLK)


def split(x):
    high = x.astype(BF16)
    return high, (x - high.astype(F32)).astype(BF16)


def mm(a, b):
    return jnp.dot(a, b, preferred_element_type=F32)


def mm_t(a, b):
    return lax.dot_general(a, b, (((0,), (0,)), ((), ())), preferred_element_type=F32)


def mm3(high, low, right_high, right_low):
    left = jnp.concatenate([high, low, high], axis=1)
    return mm(left, jnp.concatenate([right_high, right_high, right_low], axis=0))


def mm3_t(high, low, right_high, right_low):
    left = jnp.concatenate([high, low, high], axis=0)
    return mm_t(left, jnp.concatenate([right_high, right_high, right_low], axis=0))


def quad(b11, b12, b21, b22):
    top = jnp.concatenate([b11, b12], axis=1)
    return jnp.concatenate([top, jnp.concatenate([b21, b22], axis=1)], axis=0)


def wrap(value):
    return jnp.where(value >= SIDE, value - SIDE, value)


def digit(m):
    return jnp.where(m == 3, 0, jnp.where(m == 2, 3, 2 - m))


def for_the_others(z, x, y, body):
    @pl.loop(0, 2 * SIDE)
    def _(i):
        later = jnp.where(i >= SIDE, 1, 0)
        pz = jnp.where(later == z, 1, 0)
        px = wrap(x + digit(i - SIDE * later))
        base = (pz * SIDE + px) * SIDE

        @pl.loop(0, jnp.where(i == 2 * SIDE - 1, SIDE - 1, SIDE))
        def _(j):
            body(base + wrap(y + digit(j)))


def cayley_less_identity(g11, g12, g22, q, z_high, z_low):
    row = lax.broadcasted_iota(jnp.int32, (BLK, BLK), 0)
    col = lax.broadcasted_iota(jnp.int32, (BLK, BLK), 1)
    diag = row == col
    sign = jnp.where(row < col, 1.0, jnp.where(diag, 0.0, -1.0))

    def inv(x, axis):
        total = jnp.sum(jnp.where(diag, x, 0.0), axis=axis, keepdims=True)
        return 1.0 / jnp.sqrt(total + 1e-06)

    n1_row, n1_col, n2_row, n2_col = inv(g11, 0), inv(g11, 1), inv(g22, 0), inv(g22, 1)
    s12 = g12 * n1_col * n2_row
    raw = quad(
        sign * (g11 * n1_col * n1_row), s12, -s12.T, sign * (g22 * n2_col * n2_row)
    )
    sums = jnp.sum(jnp.abs(raw), axis=0, keepdims=True)
    bound = jnp.max(sums, axis=1, keepdims=True)
    skew = raw * (1.0 / (1.0 + 2.0 * bound))
    q[...] = skew
    z_high[...], z_low[...] = split(skew)

    def step(i, carry):
        q_high, q_low = split(q[...])
        high = jnp.concatenate([q_high, z_high[...]], axis=0)
        low = jnp.concatenate([q_low, z_low[...]], axis=0)
        times = mm3(high, low, z_high[...], z_low[...])
        q[...] = q[...] + (z_high[...].astype(F32) + z_low[...].astype(F32)) + times[: 2 * BLK]
        z_high[...], z_low[...] = split(times[2 * BLK :])
        return carry

    lax.fori_loop(0, NS_STEPS + 1, step, 0)


def kernel(distances, n_pos, n_rows, x_hbm, out_hbm, a, b, s, x_high, x_low, pack, part,
           full, g, known, turned, q, z_high, z_low, load_sem, in_sem, send_sem, part_send,
           part_recv, sum_send, sum_recv, e_send, e_recv, out_sem):
    me = lax.axis_index("rows")
    pos = lax.axis_index("pos")
    others = n_rows - 1
    near = NEAR
    height = a.shape[0]
    step = height // CHUNKS
    barrier = pltpu.get_barrier_semaphore()
    moves = sorted(set(distances) - {0})
    z, x, y = lax.div(me, 16), lax.rem(lax.div(me, 4), 4), lax.rem(me, 4)

    def chunk_of(cz, cx, cy):
        return wrap(cx + 2 * cz) * SIDE + wrap(cy + 2 * cz)

    load_a = pltpu.make_async_copy(x_hbm.at[:, pl.ds(0, BLK)], a, load_sem)
    load_a.start()
    for c in range(CHUNKS):
        rows = pl.ds(c * step, step)
        pltpu.make_async_copy(
            x_hbm.at[rows, pl.ds(BLK, BLK)], b.at[0, rows], in_sem.at[0, c]
        ).start()

    def greet(peer):
        pl.semaphore_signal(
            barrier, inc=1, device_id={"rows": peer}, device_id_type=MESH
        )

    for_the_others(z, x, y, greet)

    for value in moves:
        pl.semaphore_signal(
            barrier, inc=1, device_id={"pos": lax.rem(pos + n_pos - value, n_pos)},
            device_id_type=MESH,
        )

    def target(r):
        distance = COMMON
        for i, value in enumerate(distances):
            distance = jnp.where(r == i, value, distance)
        return lax.rem(pos + distance, n_pos)

    def move(r, src, dst, send, recv):
        def away():
            pltpu.make_async_remote_copy(
                src_ref=src, dst_ref=dst, send_sem=send, recv_sem=recv,
                device_id={"pos": target(r)}, device_id_type=MESH,
            ).start()

        def keep():
            pltpu.make_async_copy(src, dst, recv).start()

        if 0 in distances:
            stays = distances.index(0)
            pl.when(r == stays)(keep)
            pl.when(r != stays)(away)
        else:
            away()

    def wait(ref, sem):
        pltpu.make_async_copy(ref, ref, sem).wait()

    mine = chunk_of(z, x, y)
    my_rows = pl.ds(pl.multiple_of(mine * TILE, TILE), TILE)

    def sized(r, send):
        @pl.when(r == 0)
        def _():
            send(BLOCKS)

        @pl.when(r > 0)
        def _():
            send(1)

    def near_sends(r):
        @pl.loop(1, near + 1)
        def _(i):
            ox = lax.div(i, SIDE)
            oy = i - ox * SIDE
            distance = jnp.where(ox == 3, 1, ox) + jnp.where(oy == 3, 1, oy)
            away = jnp.where(distance > 2, 1, 0)
            pz = jnp.where(away == z, 0, 1)
            px, py = wrap(wrap(x + ox) + 2 * away), wrap(wrap(y + oy) + 2 * away)
            rows = pl.ds(pl.multiple_of(chunk_of(pz, px, py) * TILE, TILE), TILE)

            def send(blocks):
                pltpu.make_async_remote_copy(
                    src_ref=pack.at[r, pl.ds(0, blocks), rows],
                    dst_ref=part.at[r, i - 1, pl.ds(0, blocks)],
                    send_sem=part_send.at[r],
                    recv_sem=part_recv.at[r],
                    device_id={"rows": (pz * SIDE + px) * SIDE + py},
                    device_id_type=MESH,
                ).start()

            sized(r, send)

    def wait_blocks(r, count, sem):
        sized(r, lambda blocks: wait(part.at[r, pl.ds(0, count), pl.ds(0, blocks)], sem.at[r]))

    def add_and_send(r, blocks):
        wait_blocks(r, near, part_recv)

        @pl.loop(0, blocks)
        def _(k):
            terms = [pack[r, k, my_rows, :]]
            terms += [part[r, slot, k] for slot in range(near)]
            while len(terms) > 1:
                terms = [sum(terms[i : i + 2]) for i in range(0, len(terms), 2)]
            full[r, z, k, my_rows, :] = terms[0]

        def send_to(peer):
            def send(blocks):
                ref = full.at[r, z, pl.ds(0, blocks), my_rows]
                pltpu.make_async_remote_copy(
                    src_ref=ref,
                    dst_ref=ref,
                    send_sem=sum_send.at[r],
                    recv_sem=sum_recv.at[r],
                    device_id={"rows": peer},
                    device_id_type=MESH,
                ).start()

            sized(r, send)

        for_the_others(z, x, y, send_to)

    def collect(r, blocks):
        wait_blocks(r, others, sum_recv)

        @pl.loop(0, blocks)
        def _(k):
            g[r, k] = full[r, 0, k] + full[r, 1, k]

    def known_blocks(r):
        g12 = g[r - 1, 0]
        q[...] = quad(g[r - 1, 1], g12, g12.T, g[r - 1, 2])

        @pl.loop(0, 2)
        def _(h):
            half = pl.ds(pl.multiple_of(h * BLK, BLK), BLK)
            d_high, d_low = z_high[:, half], z_low[:, half]
            high, low = split(q[...])
            turned[...] = q[:, half] + mm3(high, low, d_high, d_low)
            high, low = split(turned[...])
            known[r, h] = turned[half, :] + mm3_t(d_high, d_low, high, low)

        g[r, 1] = known[r, 0]
        move(r - 1, known.at[r, 1], g.at[r, 2], e_send.at[r], e_recv.at[r])

    load_a.wait()

    @pl.loop(0, CHUNKS)
    def _(c):
        rows = pl.ds(pl.multiple_of(c * step, step), step)
        x_high[rows, FIRST], x_low[rows, FIRST] = split(a[rows, :])

    def one_round(r, carry):
        blocks = jnp.where(r == 0, BLOCKS, 1)

        @pl.loop(0, blocks)
        def _(k):
            left = pl.ds(pl.multiple_of(lax.div(k, 2) * BLK, BLK), BLK)
            right = pl.ds(pl.multiple_of((1 - lax.rem(k, 2)) * BLK, BLK), BLK)

            def add_rows(c, total):
                rows = pl.ds(pl.multiple_of(c * step, step), step)

                @pl.when(k == 0)
                def _():
                    wait(b.at[r, rows], in_sem.at[r, c])
                    x_high[rows, SECOND], x_low[rows, SECOND] = split(b[r, rows, :])

                return total + mm3_t(
                    x_high[rows, left], x_low[rows, left], x_high[rows, right], x_low[rows, right]
                )

            pack[r, k] = lax.fori_loop(0, CHUNKS, add_rows, jnp.zeros((BLK, BLK), F32))

        @pl.when(r == 0)
        def _():
            pl.semaphore_wait(barrier, others + len(moves))

        near_sends(r)

        @pl.when(r > 0)
        def _():
            known_blocks(r)

        add_and_send(r, blocks)
        collect(r, blocks)

        @pl.when(r > 0)
        def _():
            wait(g.at[r, 2], e_recv.at[r])

        cayley_less_identity(g[r, 1], g[r, 0], g[r, 2], q, z_high, z_low)
        z_high[...], z_low[...] = split(q[...])

        @pl.loop(0, CHUNKS)
        def _(c):
            rows = pl.ds(pl.multiple_of(c * step, step), step)
            new = jnp.concatenate([a[rows, :], b[r, rows, :]], axis=1) + mm3(
                x_high[rows, :], x_low[rows, :], z_high[...], z_low[...]
            )
            s[r, rows, :] = new[:, SECOND]
            move(r, s.at[r, rows], b.at[r + 1, rows], send_sem.at[r, c], in_sem.at[r + 1, c])
            a[rows, :] = new[:, FIRST]
            x_high[rows, FIRST], x_low[rows, FIRST] = split(new[:, FIRST])

        return carry

    lax.fori_loop(0, ROUNDS, one_round, 0)

    out_a = pltpu.make_async_copy(a, out_hbm.at[:, pl.ds(0, BLK)], out_sem.at[CHUNKS])
    out_a.start()

    def drain(r, blocks):
        wait(part.at[r, pl.ds(0, near), pl.ds(0, blocks)], part_send.at[r])
        wait(part.at[r, pl.ds(0, others), pl.ds(0, blocks)], sum_send.at[r])

    for r in range(ROUNDS):
        drain(r, 1 if r else BLOCKS)
        if r and distances[r - 1]:
            wait(known.at[r, 1], e_send.at[r])

    @pl.loop(0, CHUNKS)
    def _(c):
        rows = pl.ds(pl.multiple_of(c * step, step), step)
        wait(b.at[ROUNDS, rows], in_sem.at[ROUNDS, c])
        pltpu.make_async_copy(
            b.at[ROUNDS, rows], out_hbm.at[rows, pl.ds(BLK, BLK)], out_sem.at[c]
        ).start()
        for r in range(ROUNDS):
            if distances[r]:
                wait(s.at[r, rows], send_sem.at[r, c])

    for c in range(CHUNKS):
        rows = pl.ds(c * step, step)
        wait(b.at[ROUNDS, rows], out_sem.at[c])
    out_a.wait()


def make_branch(distances, identity, n_pos, n_rows, height):
    square = (2 * BLK, 2 * BLK)
    dma = pltpu.SemaphoreType.DMA
    return pl.pallas_call(
        functools.partial(kernel, distances, n_pos, n_rows),
        out_shape=jax.ShapeDtypeStruct((height, 2 * BLK), F32),
        in_specs=[pl.BlockSpec(memory_space=pl.ANY)],
        out_specs=pl.BlockSpec(memory_space=pl.ANY),
        scratch_shapes=[
            pltpu.VMEM((height, BLK), F32),
            pltpu.VMEM((ROUNDS + 1, height, BLK), F32),
            pltpu.VMEM((ROUNDS, height, BLK), F32),
            pltpu.VMEM((height, 2 * BLK), BF16),
            pltpu.VMEM((height, 2 * BLK), BF16),
            pltpu.VMEM((ROUNDS, BLOCKS, BLK, BLK), F32),
            pltpu.VMEM((ROUNDS, n_rows - 1, BLOCKS, TILE, BLK), F32),
            pltpu.VMEM((ROUNDS, 2, BLOCKS, BLK, BLK), F32),
            pltpu.VMEM((ROUNDS, BLOCKS, BLK, BLK), F32),
            pltpu.VMEM((ROUNDS, 2, BLK, BLK), F32),
            pltpu.VMEM((2 * BLK, BLK), F32),
            pltpu.VMEM(square, F32),
            pltpu.VMEM(square, BF16),
            pltpu.VMEM(square, BF16),
            dma,
            dma((ROUNDS + 1, CHUNKS)),
            dma((ROUNDS, CHUNKS)),
            dma((ROUNDS,)),
            dma((ROUNDS,)),
            dma((ROUNDS,)),
            dma((ROUNDS,)),
            dma((ROUNDS,)),
            dma((ROUNDS,)),
            dma((CHUNKS + 1,)),
        ],
        compiler_params=pltpu.CompilerParams(
            collective_id=identity, has_side_effects=True, vmem_limit_bytes=32 << 20
        ),
    )


def solution(mesh):
    n_pos, n_rows = mesh.shape["pos"], mesh.shape["rows"]
    common = COMMON % n_pos
    plans = [
        tuple(value if i == odd else common for i in range(ROUNDS))
        for odd in range(ROUNDS)
        for value in range(n_pos - 1)
    ]
    plans.append((common,) * ROUNDS)

    def shards(matrix, shifts):
        moved = jnp.bitwise_and(shifts, n_pos - 1)
        number = lax.iota(jnp.int32, ROUNDS) * (n_pos - 1) + moved
        behind = jnp.where(moved != common, len(plans) - 1 - number, 0)
        plan = len(plans) - 1 - jnp.sum(behind)
        branches = [
            make_branch(distances, i, n_pos, n_rows, matrix.shape[0])
            for i, distances in enumerate(plans)
        ]
        return lax.switch(plan, branches, matrix)

    return jax.shard_map(
        shards, mesh=mesh, in_specs=(P("rows", "pos"), P()), out_specs=P("rows", "pos"),
        check_vma=False,
    )
```

```python
import functools

import jax
import jax.numpy as jnp
from jax import lax
from jax.experimental import pallas as pl
from jax.experimental.pallas import tpu as pltpu
from jax.sharding import PartitionSpec as P

ROUNDS = 3
NS_STEPS = 3
COMMON = 7
BLK = 128
TILE = 8
CHUNKS = 2
BLOCKS = 3
SIDE = 4
NEAR = 15
MESH = pl.DeviceIdType.MESH
F32 = jnp.float32
BF16 = jnp.bfloat16
FIRST, SECOND = slice(0, BLK), slice(BLK, 2 * BLK)


def split(x):
    high = x.astype(BF16)
    return high, (x - high.astype(F32)).astype(BF16)


def mm(a, b):
    return jnp.dot(a, b, preferred_element_type=F32)


def mm_t(a, b):
    return lax.dot_general(a, b, (((0,), (0,)), ((), ())), preferred_element_type=F32)


def mm3(high, low, right_high, right_low):
    left = jnp.concatenate([high, low, high], axis=1)
    return mm(left, jnp.concatenate([right_high, right_high, right_low], axis=0))


def mm3_t(high, low, right_high, right_low):
    left = jnp.concatenate([high, low, high], axis=0)
    return mm_t(left, jnp.concatenate([right_high, right_high, right_low], axis=0))


def quad(b11, b12, b21, b22):
    top = jnp.concatenate([b11, b12], axis=1)
    return jnp.concatenate([top, jnp.concatenate([b21, b22], axis=1)], axis=0)


def wrap(value):
    return jnp.where(value >= SIDE, value - SIDE, value)


def digit(m):
    return jnp.where(m == 3, 0, jnp.where(m == 2, 3, 2 - m))


def for_the_others(z, x, y, body):
    @pl.loop(0, 2 * SIDE)
    def _(i):
        later = jnp.where(i >= SIDE, 1, 0)
        pz = jnp.where(later == z, 1, 0)
        px = wrap(x + digit(i - SIDE * later))
        base = (pz * SIDE + px) * SIDE

        @pl.loop(0, jnp.where(i == 2 * SIDE - 1, SIDE - 1, SIDE))
        def _(j):
            body(base + wrap(y + digit(j)))


def cayley_less_identity(g11, g12, g22, q, z_high, z_low):
    row = lax.broadcasted_iota(jnp.int32, (BLK, BLK), 0)
    col = lax.broadcasted_iota(jnp.int32, (BLK, BLK), 1)
    diag = row == col
    sign = jnp.where(row < col, 1.0, jnp.where(diag, 0.0, -1.0))

    def inv(x, axis):
        total = jnp.sum(jnp.where(diag, x, 0.0), axis=axis, keepdims=True)
        return 1.0 / jnp.sqrt(total + 1e-06)

    n1_row, n1_col, n2_row, n2_col = inv(g11, 0), inv(g11, 1), inv(g22, 0), inv(g22, 1)
    s12 = g12 * n1_col * n2_row
    raw = quad(
        sign * (g11 * n1_col * n1_row), s12, -s12.T, sign * (g22 * n2_col * n2_row)
    )
    sums = jnp.sum(jnp.abs(raw), axis=0, keepdims=True)
    bound = jnp.max(sums, axis=1, keepdims=True)
    skew = raw * (1.0 / (1.0 + 2.0 * bound))
    q[...] = skew
    z_high[...], z_low[...] = split(skew)

    def step(i, carry):
        q_high, q_low = split(q[...])
        high = jnp.concatenate([q_high, z_high[...]], axis=0)
        low = jnp.concatenate([q_low, z_low[...]], axis=0)
        times = mm3(high, low, z_high[...], z_low[...])
        q[...] = q[...] + (z_high[...].astype(F32) + z_low[...].astype(F32)) + times[: 2 * BLK]
        z_high[...], z_low[...] = split(times[2 * BLK :])
        return carry

    lax.fori_loop(0, NS_STEPS + 1, step, 0)


def kernel(distances, n_pos, n_rows, x_hbm, out_hbm, a, b, s, x_high, x_low, pack, part,
           full, g, known, turned, q, z_high, z_low, load_sem, in_sem, send_sem, part_send,
           part_recv, sum_send, sum_recv, e_send, e_recv, out_sem):
    me = lax.axis_index("rows")
    pos = lax.axis_index("pos")
    others = n_rows - 1
    near = NEAR
    height = a.shape[0]
    step = height // CHUNKS
    barrier = pltpu.get_barrier_semaphore()
    moves = sorted(set(distances) - {0})
    z, x, y = lax.div(me, 16), lax.rem(lax.div(me, 4), 4), lax.rem(me, 4)

    def chunk_of(cz, cx, cy):
        return wrap(cx + 2 * cz) * SIDE + wrap(cy + 2 * cz)

    load_a = pltpu.make_async_copy(x_hbm.at[:, pl.ds(0, BLK)], a, load_sem)
    load_a.start()
    for c in range(CHUNKS):
        rows = pl.ds(c * step, step)
        pltpu.make_async_copy(
            x_hbm.at[rows, pl.ds(BLK, BLK)], b.at[0, rows], in_sem.at[0, c]
        ).start()

    def greet(peer):
        pl.semaphore_signal(
            barrier, inc=1, device_id={"rows": peer}, device_id_type=MESH
        )

    for_the_others(z, x, y, greet)

    for value in moves:
        pl.semaphore_signal(
            barrier, inc=1, device_id={"pos": lax.rem(pos + n_pos - value, n_pos)},
            device_id_type=MESH,
        )

    def target(r):
        distance = COMMON
        for i, value in enumerate(distances):
            distance = jnp.where(r == i, value, distance)
        return lax.rem(pos + distance, n_pos)

    def move(r, src, dst, send, recv):
        def away():
            pltpu.make_async_remote_copy(
                src_ref=src, dst_ref=dst, send_sem=send, recv_sem=recv,
                device_id={"pos": target(r)}, device_id_type=MESH,
            ).start()

        def keep():
            pltpu.make_async_copy(src, dst, recv).start()

        if 0 in distances:
            stays = distances.index(0)
            pl.when(r == stays)(keep)
            pl.when(r != stays)(away)
        else:
            away()

    def wait(ref, sem):
        pltpu.make_async_copy(ref, ref, sem).wait()

    mine = chunk_of(z, x, y)
    my_rows = pl.ds(pl.multiple_of(mine * TILE, TILE), TILE)

    def sized(r, send):
        @pl.when(r == 0)
        def _():
            send(BLOCKS)

        @pl.when(r > 0)
        def _():
            send(1)

    layer, other_layer = z * SIDE * SIDE, (1 - z) * SIDE * SIDE
    places = [wrap(y + d) for d in range(SIDE)]
    chunk_places = [wrap(wrap(y + 2 * z) + d) * TILE for d in range(SIDE)]

    def near_sends(r):
        def send(blocks):
            @pl.loop(0, SIDE)
            def _(ox):
                distance = jnp.where(ox == 3, 1, ox)
                column = wrap(x + ox)
                here = layer + column * SIDE
                there = other_layer + wrap(column + 2) * SIDE
                chunk_column = wrap(wrap(x + 2 * z) + ox) * SIDE * TILE

                for oy in range(SIDE):

                    def start():
                        away = distance > 2 - min(oy, SIDE - oy)
                        peer = jnp.where(away, there + places[(oy + 2) % SIDE], here + places[oy])
                        row = pl.multiple_of(chunk_column + chunk_places[oy], TILE)
                        pltpu.make_async_remote_copy(
                            src_ref=pack.at[r, pl.ds(0, blocks), pl.ds(row, TILE)],
                            dst_ref=part.at[r, ox * SIDE + oy, pl.ds(0, blocks)],
                            send_sem=part_send.at[r],
                            recv_sem=part_recv.at[r],
                            device_id={"rows": peer},
                            device_id_type=MESH,
                        ).start()

                    if oy:
                        start()
                    else:
                        pl.when(ox > 0)(start)

        sized(r, send)

    def wait_blocks(r, count, sem):
        sized(r, lambda blocks: wait(part.at[r, pl.ds(0, count), pl.ds(0, blocks)], sem.at[r]))

    def add_and_send(r, blocks):
        wait_blocks(r, near, part_recv)

        @pl.loop(0, blocks)
        def _(k):
            terms = [pack[r, k, my_rows, :]]
            terms += [part[r, slot, k] for slot in range(1, near + 1)]
            while len(terms) > 1:
                terms = [sum(terms[i : i + 2]) for i in range(0, len(terms), 2)]
            full[r, z, k, my_rows, :] = terms[0]

        def send_to(peer):
            def send(blocks):
                ref = full.at[r, z, pl.ds(0, blocks), my_rows]
                pltpu.make_async_remote_copy(
                    src_ref=ref,
                    dst_ref=ref,
                    send_sem=sum_send.at[r],
                    recv_sem=sum_recv.at[r],
                    device_id={"rows": peer},
                    device_id_type=MESH,
                ).start()

            sized(r, send)

        for_the_others(z, x, y, send_to)

    def collect(r, blocks):
        wait_blocks(r, others, sum_recv)

        @pl.loop(0, blocks)
        def _(k):
            g[r, k] = full[r, 0, k] + full[r, 1, k]

    def known_blocks(r):
        g12 = g[r - 1, 0]
        q[...] = quad(g[r - 1, 1], g12, g12.T, g[r - 1, 2])

        @pl.loop(0, 2)
        def _(h):
            half = pl.ds(pl.multiple_of(h * BLK, BLK), BLK)
            d_high, d_low = z_high[:, half], z_low[:, half]
            high, low = split(q[...])
            turned[...] = q[:, half] + mm3(high, low, d_high, d_low)
            high, low = split(turned[...])
            known[r, h] = turned[half, :] + mm3_t(d_high, d_low, high, low)

        g[r, 1] = known[r, 0]
        move(r - 1, known.at[r, 1], g.at[r, 2], e_send.at[r], e_recv.at[r])

    load_a.wait()

    @pl.loop(0, CHUNKS)
    def _(c):
        rows = pl.ds(pl.multiple_of(c * step, step), step)
        x_high[rows, FIRST], x_low[rows, FIRST] = split(a[rows, :])

    def one_round(r, carry):
        blocks = jnp.where(r == 0, BLOCKS, 1)

        @pl.loop(0, blocks)
        def _(k):
            left = pl.ds(pl.multiple_of(lax.div(k, 2) * BLK, BLK), BLK)
            right = pl.ds(pl.multiple_of((1 - lax.rem(k, 2)) * BLK, BLK), BLK)

            def add_rows(c, total):
                rows = pl.ds(pl.multiple_of(c * step, step), step)

                @pl.when(k == 0)
                def _():
                    wait(b.at[r, rows], in_sem.at[r, c])
                    x_high[rows, SECOND], x_low[rows, SECOND] = split(b[r, rows, :])

                return total + mm3_t(
                    x_high[rows, left], x_low[rows, left], x_high[rows, right], x_low[rows, right]
                )

            pack[r, k] = lax.fori_loop(0, CHUNKS, add_rows, jnp.zeros((BLK, BLK), F32))

        @pl.when(r == 0)
        def _():
            pl.semaphore_wait(barrier, others + len(moves))

        near_sends(r)

        @pl.when(r > 0)
        def _():
            known_blocks(r)

        add_and_send(r, blocks)
        collect(r, blocks)

        @pl.when(r > 0)
        def _():
            wait(g.at[r, 2], e_recv.at[r])

        cayley_less_identity(g[r, 1], g[r, 0], g[r, 2], q, z_high, z_low)
        z_high[...], z_low[...] = split(q[...])

        @pl.loop(0, CHUNKS)
        def _(c):
            rows = pl.ds(pl.multiple_of(c * step, step), step)
            new = jnp.concatenate([a[rows, :], b[r, rows, :]], axis=1) + mm3(
                x_high[rows, :], x_low[rows, :], z_high[...], z_low[...]
            )
            s[r, rows, :] = new[:, SECOND]
            move(r, s.at[r, rows], b.at[r + 1, rows], send_sem.at[r, c], in_sem.at[r + 1, c])
            a[rows, :] = new[:, FIRST]
            x_high[rows, FIRST], x_low[rows, FIRST] = split(new[:, FIRST])

        return carry

    lax.fori_loop(0, ROUNDS, one_round, 0)

    out_a = pltpu.make_async_copy(a, out_hbm.at[:, pl.ds(0, BLK)], out_sem.at[CHUNKS])
    out_a.start()

    def drain(r, blocks):
        wait(part.at[r, pl.ds(0, near), pl.ds(0, blocks)], part_send.at[r])
        wait(part.at[r, pl.ds(0, others), pl.ds(0, blocks)], sum_send.at[r])

    for r in range(ROUNDS):
        drain(r, 1 if r else BLOCKS)
        if r and distances[r - 1]:
            wait(known.at[r, 1], e_send.at[r])

    @pl.loop(0, CHUNKS)
    def _(c):
        rows = pl.ds(pl.multiple_of(c * step, step), step)
        wait(b.at[ROUNDS, rows], in_sem.at[ROUNDS, c])
        pltpu.make_async_copy(
            b.at[ROUNDS, rows], out_hbm.at[rows, pl.ds(BLK, BLK)], out_sem.at[c]
        ).start()
        for r in range(ROUNDS):
            if distances[r]:
                wait(s.at[r, rows], send_sem.at[r, c])

    for c in range(CHUNKS):
        rows = pl.ds(c * step, step)
        wait(b.at[ROUNDS, rows], out_sem.at[c])
    out_a.wait()


def make_branch(distances, identity, n_pos, n_rows, height):
    square = (2 * BLK, 2 * BLK)
    dma = pltpu.SemaphoreType.DMA
    return pl.pallas_call(
        functools.partial(kernel, distances, n_pos, n_rows),
        out_shape=jax.ShapeDtypeStruct((height, 2 * BLK), F32),
        in_specs=[pl.BlockSpec(memory_space=pl.ANY)],
        out_specs=pl.BlockSpec(memory_space=pl.ANY),
        scratch_shapes=[
            pltpu.VMEM((height, BLK), F32),
            pltpu.VMEM((ROUNDS + 1, height, BLK), F32),
            pltpu.VMEM((ROUNDS, height, BLK), F32),
            pltpu.VMEM((height, 2 * BLK), BF16),
            pltpu.VMEM((height, 2 * BLK), BF16),
            pltpu.VMEM((ROUNDS, BLOCKS, BLK, BLK), F32),
            pltpu.VMEM((ROUNDS, n_rows - 1, BLOCKS, TILE, BLK), F32),
            pltpu.VMEM((ROUNDS, 2, BLOCKS, BLK, BLK), F32),
            pltpu.VMEM((ROUNDS, BLOCKS, BLK, BLK), F32),
            pltpu.VMEM((ROUNDS, 2, BLK, BLK), F32),
            pltpu.VMEM((2 * BLK, BLK), F32),
            pltpu.VMEM(square, F32),
            pltpu.VMEM(square, BF16),
            pltpu.VMEM(square, BF16),
            dma,
            dma((ROUNDS + 1, CHUNKS)),
            dma((ROUNDS, CHUNKS)),
            dma((ROUNDS,)),
            dma((ROUNDS,)),
            dma((ROUNDS,)),
            dma((ROUNDS,)),
            dma((ROUNDS,)),
            dma((ROUNDS,)),
            dma((CHUNKS + 1,)),
        ],
        compiler_params=pltpu.CompilerParams(
            collective_id=identity, has_side_effects=True, vmem_limit_bytes=32 << 20
        ),
    )


def solution(mesh):
    n_pos, n_rows = mesh.shape["pos"], mesh.shape["rows"]
    common = COMMON % n_pos
    plans = [
        tuple(value if i == odd else common for i in range(ROUNDS))
        for odd in range(ROUNDS)
        for value in range(n_pos - 1)
    ]
    plans.append((common,) * ROUNDS)

    def shards(matrix, shifts):
        moved = jnp.bitwise_and(shifts, n_pos - 1)
        number = lax.iota(jnp.int32, ROUNDS) * (n_pos - 1) + moved
        behind = jnp.where(moved != common, len(plans) - 1 - number, 0)
        plan = len(plans) - 1 - jnp.sum(behind)
        branches = [
            make_branch(distances, i, n_pos, n_rows, matrix.shape[0])
            for i, distances in enumerate(plans)
        ]
        return lax.switch(plan, branches, matrix)

    return jax.shard_map(
        shards, mesh=mesh, in_specs=(P("rows", "pos"), P()), out_specs=P("rows", "pos"),
        check_vma=False,
    )
```

```python
import functools

import jax
import jax.numpy as jnp
from jax import lax
from jax.experimental import pallas as pl
from jax.experimental.pallas import tpu as pltpu
from jax.sharding import PartitionSpec as P

ROUNDS = 3
NS_STEPS = 3
COMMON = 7
BLK = 128
TILE = 8
CHUNKS = 2
BLOCKS = 3
SIDE = 4
NEAR = 15
MESH = pl.DeviceIdType.MESH
F32 = jnp.float32
BF16 = jnp.bfloat16
FIRST, SECOND = slice(0, BLK), slice(BLK, 2 * BLK)


def split(x):
    high = x.astype(BF16)
    return high, (x - high.astype(F32)).astype(BF16)


def mm(a, b):
    return jnp.dot(a, b, preferred_element_type=F32)


def mm_t(a, b):
    return lax.dot_general(a, b, (((0,), (0,)), ((), ())), preferred_element_type=F32)


def mm3(high, low, right_high, right_low):
    left = jnp.concatenate([high, low, high], axis=1)
    return mm(left, jnp.concatenate([right_high, right_high, right_low], axis=0))


def mm3_t(high, low, right_high, right_low):
    left = jnp.concatenate([high, low, high], axis=0)
    return mm_t(left, jnp.concatenate([right_high, right_high, right_low], axis=0))


def quad(b11, b12, b21, b22):
    top = jnp.concatenate([b11, b12], axis=1)
    return jnp.concatenate([top, jnp.concatenate([b21, b22], axis=1)], axis=0)


def wrap(value):
    return jnp.where(value >= SIDE, value - SIDE, value)


def digit(m):
    return jnp.where(m == 3, 0, jnp.where(m == 2, 3, 2 - m))


def for_the_others(z, x, y, body):
    @pl.loop(0, 2 * SIDE)
    def _(i):
        later = jnp.where(i >= SIDE, 1, 0)
        pz = jnp.where(later == z, 1, 0)
        px = wrap(x + digit(i - SIDE * later))
        base = (pz * SIDE + px) * SIDE

        @pl.loop(0, jnp.where(i == 2 * SIDE - 1, SIDE - 1, SIDE))
        def _(j):
            body(base + wrap(y + digit(j)))


def cayley_less_identity(g11, g12, g22, q, z_high, z_low):
    row = lax.broadcasted_iota(jnp.int32, (BLK, BLK), 0)
    col = lax.broadcasted_iota(jnp.int32, (BLK, BLK), 1)
    diag = row == col
    sign = jnp.where(row < col, 1.0, jnp.where(diag, 0.0, -1.0))

    def inv(x, axis):
        total = jnp.sum(jnp.where(diag, x, 0.0), axis=axis, keepdims=True)
        return 1.0 / jnp.sqrt(total + 1e-06)

    n1_row, n1_col, n2_row, n2_col = inv(g11, 0), inv(g11, 1), inv(g22, 0), inv(g22, 1)
    s12 = g12 * n1_col * n2_row
    raw = quad(
        sign * (g11 * n1_col * n1_row), s12, -s12.T, sign * (g22 * n2_col * n2_row)
    )
    sums = jnp.sum(jnp.abs(raw), axis=0, keepdims=True)
    bound = jnp.max(sums, axis=1, keepdims=True)
    skew = raw * (1.0 / (1.0 + 2.0 * bound))
    q[...] = skew
    z_high[...], z_low[...] = split(skew)

    def step(i, carry):
        q_high, q_low = split(q[...])
        high = jnp.concatenate([q_high, z_high[...]], axis=0)
        low = jnp.concatenate([q_low, z_low[...]], axis=0)
        times = mm3(high, low, z_high[...], z_low[...])
        q[...] = q[...] + (z_high[...].astype(F32) + z_low[...].astype(F32)) + times[: 2 * BLK]
        z_high[...], z_low[...] = split(times[2 * BLK :])
        return carry

    lax.fori_loop(0, NS_STEPS + 1, step, 0)


def kernel(distances, n_pos, n_rows, x_hbm, out_hbm, a, b, s, x_high, x_low, pack, part,
           full, g, known, turned, q, z_high, z_low, load_sem, in_sem, send_sem, part_send,
           part_recv, sum_send, sum_recv, e_send, e_recv, out_sem):
    me = lax.axis_index("rows")
    pos = lax.axis_index("pos")
    others = n_rows - 1
    near = NEAR
    height = a.shape[0]
    step = height // CHUNKS
    barrier = pltpu.get_barrier_semaphore()
    moves = sorted(set(distances) - {0})
    z, x, y = lax.div(me, 16), lax.rem(lax.div(me, 4), 4), lax.rem(me, 4)

    def chunk_of(cz, cx, cy):
        return wrap(cx + 2 * cz) * SIDE + wrap(cy + 2 * cz)

    load_a = pltpu.make_async_copy(x_hbm.at[:, pl.ds(0, BLK)], a, load_sem)
    load_a.start()
    for c in range(CHUNKS):
        rows = pl.ds(c * step, step)
        pltpu.make_async_copy(
            x_hbm.at[rows, pl.ds(BLK, BLK)], b.at[0, rows], in_sem.at[0, c]
        ).start()

    def greet(peer):
        pl.semaphore_signal(
            barrier, inc=1, device_id={"rows": peer}, device_id_type=MESH
        )

    @pl.loop(1, near + 1)
    def _(i):
        ox = lax.div(i, SIDE)
        oy = i - ox * SIDE
        distance = jnp.where(ox == 3, 1, ox) + jnp.where(oy == 3, 1, oy)
        away = jnp.where(distance > 2, 1, 0)
        pz = jnp.where(away == z, 0, 1)
        px, py = wrap(wrap(x + ox) + 2 * away), wrap(wrap(y + oy) + 2 * away)
        greet((pz * SIDE + px) * SIDE + py)

    greet(((1 - z) * SIDE + wrap(x + 1)) * SIDE + wrap(y + 1))

    for value in moves:
        pl.semaphore_signal(
            barrier, inc=1, device_id={"pos": lax.rem(pos + n_pos - value, n_pos)},
            device_id_type=MESH,
        )

    def target(r):
        distance = COMMON
        for i, value in enumerate(distances):
            distance = jnp.where(r == i, value, distance)
        return lax.rem(pos + distance, n_pos)

    def move(r, src, dst, send, recv):
        def away():
            pltpu.make_async_remote_copy(
                src_ref=src, dst_ref=dst, send_sem=send, recv_sem=recv,
                device_id={"pos": target(r)}, device_id_type=MESH,
            ).start()

        def keep():
            pltpu.make_async_copy(src, dst, recv).start()

        if 0 in distances:
            stays = distances.index(0)
            pl.when(r == stays)(keep)
            pl.when(r != stays)(away)
        else:
            away()

    def wait(ref, sem):
        pltpu.make_async_copy(ref, ref, sem).wait()

    mine = chunk_of(z, x, y)
    my_rows = pl.ds(pl.multiple_of(mine * TILE, TILE), TILE)

    def sized(r, send):
        @pl.when(r == 0)
        def _():
            send(BLOCKS)

        @pl.when(r > 0)
        def _():
            send(1)

    layer, other_layer = z * SIDE * SIDE, (1 - z) * SIDE * SIDE
    places = [wrap(y + d) for d in range(SIDE)]
    chunk_places = [wrap(wrap(y + 2 * z) + d) * TILE for d in range(SIDE)]

    def near_sends(r):
        def send(blocks):
            @pl.loop(0, SIDE)
            def _(ox):
                distance = jnp.where(ox == 3, 1, ox)
                column = wrap(x + ox)
                here = layer + column * SIDE
                there = other_layer + wrap(column + 2) * SIDE
                chunk_column = wrap(wrap(x + 2 * z) + ox) * SIDE * TILE

                for oy in range(SIDE):

                    def start():
                        away = distance > 2 - min(oy, SIDE - oy)
                        peer = jnp.where(away, there + places[(oy + 2) % SIDE], here + places[oy])
                        row = pl.multiple_of(chunk_column + chunk_places[oy], TILE)
                        pltpu.make_async_remote_copy(
                            src_ref=pack.at[r, pl.ds(0, blocks), pl.ds(row, TILE)],
                            dst_ref=part.at[r, ox * SIDE + oy, pl.ds(0, blocks)],
                            send_sem=part_send.at[r],
                            recv_sem=part_recv.at[r],
                            device_id={"rows": peer},
                            device_id_type=MESH,
                        ).start()

                    if oy:
                        start()
                    else:
                        pl.when(ox > 0)(start)

        sized(r, send)

    def wait_blocks(r, count, sem):
        sized(r, lambda blocks: wait(part.at[r, pl.ds(0, count), pl.ds(0, blocks)], sem.at[r]))

    def add_and_send(r, blocks):
        wait_blocks(r, near, part_recv)

        @pl.loop(0, blocks)
        def _(k):
            terms = [pack[r, k, my_rows, :]]
            terms += [part[r, slot, k] for slot in range(1, near + 1)]
            while len(terms) > 1:
                terms = [sum(terms[i : i + 2]) for i in range(0, len(terms), 2)]
            full[r, z, k, my_rows, :] = terms[0]

        def send_to(peer):
            def send(blocks):
                ref = full.at[r, z, pl.ds(0, blocks), my_rows]
                pltpu.make_async_remote_copy(
                    src_ref=ref,
                    dst_ref=ref,
                    send_sem=sum_send.at[r],
                    recv_sem=sum_recv.at[r],
                    device_id={"rows": peer},
                    device_id_type=MESH,
                ).start()

            sized(r, send)

        for_the_others(z, x, y, send_to)

    def collect(r, blocks):
        wait_blocks(r, others, sum_recv)

        @pl.loop(0, blocks)
        def _(k):
            g[r, k] = full[r, 0, k] + full[r, 1, k]

    def known_blocks(r):
        g12 = g[r - 1, 0]
        q[...] = quad(g[r - 1, 1], g12, g12.T, g[r - 1, 2])

        @pl.loop(0, 2)
        def _(h):
            half = pl.ds(pl.multiple_of(h * BLK, BLK), BLK)
            d_high, d_low = z_high[:, half], z_low[:, half]
            high, low = split(q[...])
            turned[...] = q[:, half] + mm3(high, low, d_high, d_low)
            high, low = split(turned[...])
            known[r, h] = turned[half, :] + mm3_t(d_high, d_low, high, low)

        g[r, 1] = known[r, 0]
        move(r - 1, known.at[r, 1], g.at[r, 2], e_send.at[r], e_recv.at[r])

    load_a.wait()

    @pl.loop(0, CHUNKS)
    def _(c):
        rows = pl.ds(pl.multiple_of(c * step, step), step)
        x_high[rows, FIRST], x_low[rows, FIRST] = split(a[rows, :])

    def one_round(r, carry):
        blocks = jnp.where(r == 0, BLOCKS, 1)

        @pl.loop(0, blocks)
        def _(k):
            left = pl.ds(pl.multiple_of(lax.div(k, 2) * BLK, BLK), BLK)
            right = pl.ds(pl.multiple_of((1 - lax.rem(k, 2)) * BLK, BLK), BLK)

            def add_rows(c, total):
                rows = pl.ds(pl.multiple_of(c * step, step), step)

                @pl.when(k == 0)
                def _():
                    wait(b.at[r, rows], in_sem.at[r, c])
                    x_high[rows, SECOND], x_low[rows, SECOND] = split(b[r, rows, :])

                return total + mm3_t(
                    x_high[rows, left], x_low[rows, left], x_high[rows, right], x_low[rows, right]
                )

            pack[r, k] = lax.fori_loop(0, CHUNKS, add_rows, jnp.zeros((BLK, BLK), F32))

        @pl.when(r == 0)
        def _():
            pl.semaphore_wait(barrier, near + 1 + len(moves))

        near_sends(r)

        @pl.when(r > 0)
        def _():
            known_blocks(r)

        add_and_send(r, blocks)
        collect(r, blocks)

        @pl.when(r > 0)
        def _():
            wait(g.at[r, 2], e_recv.at[r])

        cayley_less_identity(g[r, 1], g[r, 0], g[r, 2], q, z_high, z_low)
        z_high[...], z_low[...] = split(q[...])

        @pl.loop(0, CHUNKS)
        def _(c):
            rows = pl.ds(pl.multiple_of(c * step, step), step)
            new = jnp.concatenate([a[rows, :], b[r, rows, :]], axis=1) + mm3(
                x_high[rows, :], x_low[rows, :], z_high[...], z_low[...]
            )
            s[r, rows, :] = new[:, SECOND]
            move(r, s.at[r, rows], b.at[r + 1, rows], send_sem.at[r, c], in_sem.at[r + 1, c])
            a[rows, :] = new[:, FIRST]
            x_high[rows, FIRST], x_low[rows, FIRST] = split(new[:, FIRST])

        return carry

    lax.fori_loop(0, ROUNDS, one_round, 0)

    out_a = pltpu.make_async_copy(a, out_hbm.at[:, pl.ds(0, BLK)], out_sem.at[CHUNKS])
    out_a.start()

    def drain(r, blocks):
        wait(part.at[r, pl.ds(0, near), pl.ds(0, blocks)], part_send.at[r])
        wait(part.at[r, pl.ds(0, others), pl.ds(0, blocks)], sum_send.at[r])

    for r in range(ROUNDS):
        drain(r, 1 if r else BLOCKS)
        if r and distances[r - 1]:
            wait(known.at[r, 1], e_send.at[r])

    @pl.loop(0, CHUNKS)
    def _(c):
        rows = pl.ds(pl.multiple_of(c * step, step), step)
        wait(b.at[ROUNDS, rows], in_sem.at[ROUNDS, c])
        pltpu.make_async_copy(
            b.at[ROUNDS, rows], out_hbm.at[rows, pl.ds(BLK, BLK)], out_sem.at[c]
        ).start()
        for r in range(ROUNDS):
            if distances[r]:
                wait(s.at[r, rows], send_sem.at[r, c])

    for c in range(CHUNKS):
        rows = pl.ds(c * step, step)
        wait(b.at[ROUNDS, rows], out_sem.at[c])
    out_a.wait()


def make_branch(distances, identity, n_pos, n_rows, height):
    square = (2 * BLK, 2 * BLK)
    dma = pltpu.SemaphoreType.DMA
    return pl.pallas_call(
        functools.partial(kernel, distances, n_pos, n_rows),
        out_shape=jax.ShapeDtypeStruct((height, 2 * BLK), F32),
        in_specs=[pl.BlockSpec(memory_space=pl.ANY)],
        out_specs=pl.BlockSpec(memory_space=pl.ANY),
        scratch_shapes=[
            pltpu.VMEM((height, BLK), F32),
            pltpu.VMEM((ROUNDS + 1, height, BLK), F32),
            pltpu.VMEM((ROUNDS, height, BLK), F32),
            pltpu.VMEM((height, 2 * BLK), BF16),
            pltpu.VMEM((height, 2 * BLK), BF16),
            pltpu.VMEM((ROUNDS, BLOCKS, BLK, BLK), F32),
            pltpu.VMEM((ROUNDS, n_rows - 1, BLOCKS, TILE, BLK), F32),
            pltpu.VMEM((ROUNDS, 2, BLOCKS, BLK, BLK), F32),
            pltpu.VMEM((ROUNDS, BLOCKS, BLK, BLK), F32),
            pltpu.VMEM((ROUNDS, 2, BLK, BLK), F32),
            pltpu.VMEM((2 * BLK, BLK), F32),
            pltpu.VMEM(square, F32),
            pltpu.VMEM(square, BF16),
            pltpu.VMEM(square, BF16),
            dma,
            dma((ROUNDS + 1, CHUNKS)),
            dma((ROUNDS, CHUNKS)),
            dma((ROUNDS,)),
            dma((ROUNDS,)),
            dma((ROUNDS,)),
            dma((ROUNDS,)),
            dma((ROUNDS,)),
            dma((ROUNDS,)),
            dma((CHUNKS + 1,)),
        ],
        compiler_params=pltpu.CompilerParams(
            collective_id=identity, has_side_effects=True, vmem_limit_bytes=32 << 20
        ),
    )


def solution(mesh):
    n_pos, n_rows = mesh.shape["pos"], mesh.shape["rows"]
    common = COMMON % n_pos
    plans = [
        tuple(value if i == odd else common for i in range(ROUNDS))
        for odd in range(ROUNDS)
        for value in range(n_pos - 1)
    ]
    plans.append((common,) * ROUNDS)

    def shards(matrix, shifts):
        moved = jnp.bitwise_and(shifts, n_pos - 1)
        number = lax.iota(jnp.int32, ROUNDS) * (n_pos - 1) + moved
        behind = jnp.where(moved != common, len(plans) - 1 - number, 0)
        plan = len(plans) - 1 - jnp.sum(behind)
        branches = [
            make_branch(distances, i, n_pos, n_rows, matrix.shape[0])
            for i, distances in enumerate(plans)
        ]
        return lax.switch(plan, branches, matrix)

    return jax.shard_map(
        shards, mesh=mesh, in_specs=(P("rows", "pos"), P()), out_specs=P("rows", "pos"),
        check_vma=False,
    )
```
